32 devices in a mesh: rows: 8 (over z, y), cols: 4 (over x, core).
Axes of the slice: x: 2, y: 2, z: 4, core: 2. Of those that a mesh axis runs over, the one named last changes fastest.
Arguments:
- eigenvectors: float32 [2, 4096, 1536], P(None, 'rows', 'cols'), may hold values from -6 to 6
- reflectors: float32 [8, 4, 2, 512, 256], P('rows', None, None, 'cols'), may hold values from -0.1875 to 0.1875
- tri_factors: float32 [8, 4, 2, 256, 256], P('rows', None, None, 'cols'), may hold values from -0.1875 to 0.1875
- block_order: int32 [8, 4], P('rows'), may hold values from 0 to 3, each once within a row
Outputs:
- transformed: float32 [2, 4096, 1536], P(None, 'rows', 'cols')
The draws below stay inside these ranges and needn't reach their ends.
Inputs may be any that keep to these rules, and one draw needn't show every extreme that they name: `block_order`: each row names the stored blocks 0 to 3 once each.
All inputs are finite; a program needn't handle non-finite values.
Results may differ from the reference program's by a relative error of at most 0.00011.
Values sent between devices are 32-bit elements; how exact they have to be, the bound alone decides.
No kernel may reach another device: no remote copies, remote signals or barrier semaphores. Data moves between devices by JAX's collectives and lax.ppermute only.
A program may use at most 64 MiB of HBM per device.

```python
import jax
import jax.numpy as jnp
from jax import lax

BAND = 256
WIN = 512
TICKS = 4
ROWS = 4096
EIGS = 1536
N_ROWS = 8


def levels(own_key, dims, pieces, low, largest):
    level = 1.0
    for axis_at, shards_of in pieces:
        steps = jax.random.uniform(jax.random.fold_in(jax.random.fold_in(own_key, 6), axis_at), (shards_of,), jnp.float32, low / len(pieces), largest / len(pieces))
        level = level * jnp.repeat(jnp.exp(steps), dims[axis_at] // shards_of).reshape((-1,) + (1,) * (len(dims) - 1 - axis_at))
    return level


def centred(own_key, extent, spread, bound, split=(), dtype=jnp.bfloat16):
    factor_of = levels(own_key, extent, split, -0.22, 0.18) if split else 1.0
    values = jax.random.normal(own_key, extent, jnp.float32) * spread * factor_of
    return jnp.minimum(jnp.maximum(values, -bound), bound).astype(dtype)


def setup_inputs(seed: int = 0) -> dict:
    streams_of = jax.random.split(jax.random.key(seed), 5)
    return {
        "eigenvectors": centred(streams_of[0], (2, ROWS, EIGS), 1.0, 6.0, ((1, 8), (2, 4)), jnp.float32),
        "reflectors": centred(streams_of[1], (N_ROWS, TICKS, 2, WIN, BAND), (2 * WIN) ** -0.5, 0.1875, ((0, 8), (3, 4)), jnp.float32),
        "tri_factors": centred(streams_of[2], (N_ROWS, TICKS, 2, BAND, BAND), (4 * BAND) ** -0.5, 0.1875, ((0, 8), (3, 4)), jnp.float32),
        "block_order": jax.vmap(lambda own: jax.random.permutation(own, TICKS))(jax.random.split(streams_of[3], N_ROWS)).reshape((N_ROWS, TICKS)).astype(jnp.int32),
    }


def complex_product(left_re, left_im, right_re, right_im, form):
    first = jnp.einsum(form, left_re, right_re, precision=lax.Precision.HIGHEST)
    second = jnp.einsum(form, left_im, right_im, precision=lax.Precision.HIGHEST)
    third = jnp.einsum(form, left_re + left_im, right_re + right_im, precision=lax.Precision.HIGHEST)
    return first - second, third - first - second


def apply_block(window, vectors, factor):
    w_re, w_im = complex_product(vectors[0], -vectors[1], window[0], window[1], "sk,se->ke")
    u_re, u_im = complex_product(factor[0], factor[1], w_re, w_im, "jk,ke->je")
    d_re, d_im = complex_product(vectors[0], vectors[1], u_re, u_im, "sk,ke->se")
    return jnp.stack([window[0] - d_re, window[1] - d_im])


def reference(eigenvectors, reflectors, tri_factors, block_order):
    width = reflectors.shape[3]
    band = reflectors.shape[4]
    ticks = reflectors.shape[1]
    sections = reflectors.shape[0]
    total = eigenvectors.shape[2]
    upper = jnp.triu(jnp.ones((band, band), jnp.float32))
    batched = jax.vmap(apply_block)
    current = eigenvectors
    for tick in range(ticks):
        chosen = block_order[:, tick]
        vectors = reflectors[jnp.arange(sections), chosen]
        factors = tri_factors[jnp.arange(sections), chosen] * upper
        if tick % 2 == 0:
            blocks = current.reshape(2, sections, width, total).transpose(1, 0, 2, 3)
            blocks = batched(blocks, vectors, factors)
            current = blocks.transpose(1, 0, 2, 3).reshape(2, sections * width, total)
        else:
            middle = current[:, band:band + (sections - 1) * width]
            blocks = middle.reshape(2, sections - 1, width, total).transpose(1, 0, 2, 3)
            blocks = batched(blocks, vectors[:sections - 1], factors[:sections - 1])
            middle = blocks.transpose(1, 0, 2, 3).reshape(2, (sections - 1) * width, total)
            current = jnp.concatenate([current[:, :band], middle, current[:, band + (sections - 1) * width:]], axis=1)
    return current
```

```python
import functools

import jax
import jax.numpy as jnp
from jax import lax
from jax.experimental import pallas as pl
from jax.experimental.pallas import tpu as pltpu
from jax.sharding import PartitionSpec as P

LANES = 128
BF16 = jnp.bfloat16
F32 = jnp.float32


def split(x):
    hi = x.astype(BF16)
    return hi, (x - hi.astype(F32)).astype(BF16)


VMEM = pl.BlockSpec(memory_space=pltpu.VMEM)
SMEM = pl.BlockSpec(memory_space=pltpu.SMEM)
HBM = pl.BlockSpec(memory_space=pl.ANY)


def limit(mib):
    return pltpu.CompilerParams(vmem_limit_bytes=mib << 20)


def pack_kernel(ticks, order_ref, v_ref, f_ref, *refs):
    outs, sem = refs[:-1], refs[-1]
    rows = v_ref.shape[3]
    copies = []
    for t, out in zip(ticks, outs):
        k = order_ref[0, t]
        copies.append(pltpu.make_async_copy(v_ref.at[0, k], out.at[:, :rows], sem.at[len(copies)]))
        copies.append(pltpu.make_async_copy(f_ref.at[0, k], out.at[:, rows:], sem.at[len(copies)]))
    for copy in copies:
        copy.start()
    for copy in copies:
        copy.wait()


def pack(order, reflectors, tri_factors, ticks):
    _, _, two, v_rows, band = reflectors.shape
    f_rows = tri_factors.shape[3]
    shape = (two, v_rows + f_rows, band)
    return pl.pallas_call(
        functools.partial(pack_kernel, ticks),
        in_specs=[SMEM, HBM, HBM],
        out_specs=[VMEM for _ in ticks],
        out_shape=[jax.ShapeDtypeStruct(shape, F32) for _ in ticks],
        scratch_shapes=[pltpu.SemaphoreType.DMA((2 * len(ticks),))],
        compiler_params=limit(1),
        name="pack",
    )(order, reflectors, tri_factors)


def prep_kernel(offsets, v_rows, q_ref, *refs):
    pieces, (vt_ref, vd_ref, ff_ref) = refs[: len(offsets)], refs[len(offsets) :]
    half = vd_ref.shape[0] // 2
    band = ff_ref.shape[0] // 2
    f_rows = pieces[0].shape[1] - v_rows
    q = q_ref[0]
    for offset, piece in zip(offsets, pieces):
        shard = lax.bitwise_xor(q, offset)
        v_at = pl.multiple_of(shard * v_rows, v_rows)
        f_at = pl.multiple_of(shard * f_rows, f_rows)
        row = f_at + lax.broadcasted_iota(jnp.int32, (f_rows, band), 0)
        upper = lax.broadcasted_iota(jnp.int32, (f_rows, band), 1) >= row
        for part in range(2):
            lanes = slice(part * band, (part + 1) * band)
            hi, lo = split(piece[part, :v_rows])
            vd_ref[pl.ds(v_at, v_rows), lanes] = hi
            vd_ref[pl.ds(half + v_at, v_rows), lanes] = lo
            hi, lo = split(jnp.where(upper, piece[part, v_rows:], 0.0))
            ff_ref[pl.ds(f_at, f_rows), lanes] = hi
            ff_ref[pl.ds(band + f_at, f_rows), lanes] = lo
    for level in range(2):
        for part in range(2):
            block = vd_ref[level * half : (level + 1) * half, part * band : (part + 1) * band]
            vt_ref[level * band : (level + 1) * band, part * half : (part + 1) * half] = block.T


def prep(q, pieces, offsets, v_rows):
    two, rows, band = pieces[0].shape
    half = v_rows * len(pieces)
    shapes = [(2 * band, 2 * half), (2 * half, 2 * band), (2 * band, 2 * band)]
    return pl.pallas_call(
        functools.partial(prep_kernel, offsets, v_rows),
        in_specs=[SMEM] + [VMEM for _ in pieces],
        out_specs=[VMEM for _ in shapes],
        out_shape=[jax.ShapeDtypeStruct(s, BF16) for s in shapes],
        compiler_params=limit(2),
        name="prep",
    )(q, *pieces)


def times(left_ref, right):
    rows = left_ref.shape[0] // 2
    hi, lo = split(right)
    both = jnp.dot(left_ref[...], hi, preferred_element_type=F32)
    return both[:rows] + both[rows:] + jnp.dot(left_ref[:rows], lo, preferred_element_type=F32)


def tick_kernel(guard_top, guard_all, chunk, section_ref, *refs):
    if guard_top:
        own_ref, *refs = refs
    top_ref, low_ref, vt_ref, vd_ref, ff_ref, *refs = refs
    top_out, low_out = refs[-2:]
    section = section_ref[0]
    if chunk is not None:
        rows = top_out.shape[1]
        lanes = slice(chunk * LANES, (chunk + 1) * LANES)
        top, low = top_ref[:, :rows, lanes], low_ref[:, rows:, lanes]
    else:
        top, low = top_ref[...], low_ref[...]
    if guard_top:
        top = jnp.where(section > 0, top, own_ref[...])
    rows, lanes = top.shape[1:]
    re = jnp.concatenate([top[0], low[0]], axis=0)
    im = jnp.concatenate([top[1], low[1]], axis=0)
    w = times(
        vt_ref,
        jnp.concatenate(
            [jnp.concatenate([re, im], axis=1), jnp.concatenate([im, -re], axis=1)], axis=0
        ),
    )

    def rotate(x):
        return jnp.concatenate(
            [x, jnp.concatenate([-x[:, lanes:], x[:, :lanes]], axis=1)], axis=0
        )

    u = times(ff_ref, rotate(w))
    d = times(vd_ref, rotate(u))
    if guard_all:
        d = jnp.where(section < section_ref[1] - 1, d, 0.0)
    top_out[0] = top[0] - d[:rows, :lanes]
    top_out[1] = top[1] - d[:rows, lanes:]
    low_out[0] = low[0] - d[rows:, :lanes]
    low_out[1] = low[1] - d[rows:, lanes:]


def tick_call(name, section, factors, top, low, own=None, guard_all=False, chunk=None, rows=None):
    shape = top.shape if chunk is None else (2, rows, LANES)
    guard = own is not None
    flops = 2 * shape[2] * 2 * sum(3 * f.size // 2 for f in factors)
    return pl.pallas_call(
        functools.partial(tick_kernel, guard, guard_all, chunk),
        in_specs=[SMEM] + [VMEM] * (5 + guard),
        out_specs=[VMEM] * 2,
        out_shape=[jax.ShapeDtypeStruct(shape, F32)] * 2,
        cost_estimate=pl.CostEstimate(
            flops=flops, transcendentals=0, bytes_accessed=sum(f.size * 2 for f in factors)
        ),
        compiler_params=limit(8),
        name=name,
    )(section, *([own] if guard else []), top, low, *factors)


def from_behind(block, distance):
    devices = range(lax.axis_size("rows"))
    route = [(i - distance, i) for i in devices if i - distance in devices]
    return lax.ppermute(block, "rows", route)


def exchange(block, mask):
    return lax.ppermute(block, "cols", [(i, i ^ mask) for i in range(lax.axis_size("cols"))])


def shards(eigenvectors, reflectors, tri_factors, block_order):
    ticks = reflectors.shape[1]
    v_rows = reflectors.shape[3]
    band = reflectors.shape[4]
    chunks = eigenvectors.shape[2] // LANES
    sections = lax.axis_size("rows")
    members = lax.axis_size("cols")
    q = lax.axis_index("cols").astype(jnp.int32).reshape(1)
    me = lax.axis_index("rows").astype(jnp.int32)
    section = jnp.stack([me, jnp.int32(sections)])

    packed = pack(block_order, reflectors, tri_factors, [0])
    packed += pack(block_order, reflectors, tri_factors, list(range(1, ticks)))
    masks = [1 << b for b in reversed(range(members.bit_length() - 1))]
    factors = []
    for tick in range(ticks):
        pieces, offsets = [packed[tick]], [0]
        for mask in masks:
            pieces = pieces + [exchange(p, mask) for p in pieces]
            offsets = offsets + [o ^ mask for o in offsets]
        factors.append(prep(q, pieces, offsets, v_rows))

    heads, tails = [None] * chunks, [None] * chunks
    given = [None] * chunks
    for tick in range(ticks):
        for c in range(chunks):
            if tick == 0:
                heads[c], tails[c] = tick_call(
                    f"tick{tick}", section, factors[tick], eigenvectors, eigenvectors, chunk=c, rows=band
                )
            elif tick % 2 == 0:
                heads[c], tails[c] = tick_call(
                    f"tick{tick}", section, factors[tick], given[c], tails[c], own=heads[c]
                )
            else:
                tails[c], back = tick_call(
                    f"tick{tick}", section, factors[tick], tails[c], given[c], guard_all=True
                )
            if tick % 2 == 0:
                given[c] = from_behind(heads[c], -1)
            else:
                given[c] = from_behind(back, 1)
    if ticks % 2 == 0:
        heads = [jnp.where(me > 0, g, h) for g, h in zip(given, heads)]
    return jnp.concatenate(
        [jnp.concatenate([h, t], axis=1) for h, t in zip(heads, tails)], axis=2
    )


def solution(mesh):
    return jax.shard_map(
        shards,
        mesh=mesh,
        in_specs=(
            P(None, "rows", "cols"),
            P("rows", None, None, "cols", None),
            P("rows", None, None, "cols", None),
            P("rows", None),
        ),
        out_specs=P(None, "rows", "cols"),
        check_vma=False,
    )
```

```python
import functools

import jax
import jax.numpy as jnp
from jax import lax
from jax.experimental import pallas as pl
from jax.experimental.pallas import tpu as pltpu
from jax.sharding import PartitionSpec as P

LANES = 128
BF16 = jnp.bfloat16
F32 = jnp.float32


def split(x):
    hi = x.astype(BF16)
    return hi, (x - hi.astype(F32)).astype(BF16)


VMEM = pl.BlockSpec(memory_space=pltpu.VMEM)
HBM = pl.BlockSpec(memory_space=pltpu.HBM)


def limit(mib):
    return pltpu.CompilerParams(vmem_limit_bytes=mib << 20)


def pack_kernel(groups, order_hbm, v_ref, f_ref, *refs):
    outs, (order_ref, order_sem, sem) = refs[:-3], refs[-3:]
    rows = v_ref.shape[3]
    fetch = pltpu.make_async_copy(order_hbm, order_ref, order_sem)
    fetch.start()
    fetch.wait()
    copies = []
    for group, out in zip(groups, outs):
        for at, t in enumerate(group):
            k = order_ref[0, t]
            for source, part in ((v_ref, slice(0, rows)), (f_ref, slice(rows, None))):
                copies.append(
                    pltpu.make_async_copy(
                        source.at[0, k], out.at[at, :, part], sem.at[len(copies)]
                    )
                )
    for copy in copies:
        copy.start()
    for copy in copies:
        copy.wait()


def pack(order, reflectors, tri_factors, groups):
    _, _, two, v_rows, band = reflectors.shape
    shape = (two, v_rows + tri_factors.shape[3], band)
    return pl.pallas_call(
        functools.partial(pack_kernel, groups),
        in_specs=[HBM, HBM, HBM],
        out_specs=[VMEM for _ in groups],
        out_shape=[jax.ShapeDtypeStruct((len(g), *shape), F32) for g in groups],
        scratch_shapes=[
            pltpu.SMEM(order.shape, jnp.int32),
            pltpu.SemaphoreType.DMA,
            pltpu.SemaphoreType.DMA((2 * sum(map(len, groups)),)),
        ],
        compiler_params=limit(1),
        name="pack",
    )(*(pltpu.with_memory_space_constraint(x, pltpu.HBM) for x in (order, reflectors, tri_factors)))


def prep_kernel(places, v_rows, *refs):
    pieces, (vt_ref, vd_ref, ff_ref) = refs[: len(places)], refs[len(places) :]
    half = vd_ref.shape[0] // 2
    band = ff_ref.shape[0] // 2
    f_rows = pieces[0].shape[2] - v_rows
    me = lax.axis_index("cols")
    for (offset, at), piece in zip(places, pieces):
        shard = lax.bitwise_xor(me, offset)
        v_at = pl.multiple_of(shard * v_rows, v_rows)
        f_at = pl.multiple_of(shard * f_rows, f_rows)
        row = f_at + lax.broadcasted_iota(jnp.int32, (f_rows, band), 0)
        upper = lax.broadcasted_iota(jnp.int32, (f_rows, band), 1) >= row
        for part in range(2):
            lanes = slice(part * band, (part + 1) * band)
            hi, lo = split(piece[at, part, :v_rows])
            vd_ref[pl.ds(v_at, v_rows), lanes] = hi
            vd_ref[pl.ds(half + v_at, v_rows), lanes] = lo
            hi, lo = split(jnp.where(upper, piece[at, part, v_rows:], 0.0))
            ff_ref[pl.ds(f_at, f_rows), lanes] = hi
            ff_ref[pl.ds(band + f_at, f_rows), lanes] = lo
    for level in range(2):
        for part in range(2):
            block = vd_ref[level * half : (level + 1) * half, part * band : (part + 1) * band]
            vt_ref[level * band : (level + 1) * band, part * half : (part + 1) * half] = block.T


def prep(pieces, places, v_rows):
    band = pieces[0].shape[3]
    half = v_rows * len(pieces)
    shapes = [(2 * band, 2 * half), (2 * half, 2 * band), (2 * band, 2 * band)]
    return pl.pallas_call(
        functools.partial(prep_kernel, places, v_rows),
        in_specs=[VMEM for _ in pieces],
        out_specs=[VMEM for _ in shapes],
        out_shape=[jax.ShapeDtypeStruct(s, BF16) for s in shapes],
        compiler_params=limit(2),
        name="prep",
    )(*pieces)


def times(left_ref, right):
    rows = left_ref.shape[0] // 2
    hi, lo = split(right)
    both = jnp.dot(left_ref[...], hi, preferred_element_type=F32)
    return both[:rows] + both[rows:] + jnp.dot(left_ref[:rows], lo, preferred_element_type=F32)


def tick_kernel(guard_top, guard_all, chunk, *refs):
    if guard_top:
        own_ref, *refs = refs
    top_ref, low_ref, vt_ref, vd_ref, ff_ref, *refs = refs
    top_out, low_out = refs[-2:]
    section = lax.axis_index("rows")
    if chunk is not None:
        rows = top_out.shape[1]
        lanes = slice(chunk * LANES, (chunk + 1) * LANES)
        top, low = top_ref[:, :rows, lanes], low_ref[:, rows:, lanes]
    else:
        top, low = top_ref[...], low_ref[...]
    if guard_top:
        top = jnp.where(section > 0, top, own_ref[...])
    rows, lanes = top.shape[1:]
    re = jnp.concatenate([top[0], low[0]], axis=0)
    im = jnp.concatenate([top[1], low[1]], axis=0)
    w = times(
        vt_ref,
        jnp.concatenate(
            [jnp.concatenate([re, im], axis=1), jnp.concatenate([im, -re], axis=1)], axis=0
        ),
    )

    def rotate(x):
        return jnp.concatenate(
            [x, jnp.concatenate([-x[:, lanes:], x[:, :lanes]], axis=1)], axis=0
        )

    u = times(ff_ref, rotate(w))
    d = times(vd_ref, rotate(u))
    if guard_all:
        d = jnp.where(section < lax.axis_size("rows") - 1, d, 0.0)
    top_out[0] = top[0] - d[:rows, :lanes]
    top_out[1] = top[1] - d[:rows, lanes:]
    low_out[0] = low[0] - d[rows:, :lanes]
    low_out[1] = low[1] - d[rows:, lanes:]


def tick_call(factors, top, low, own=None, guard_all=False, chunk=None, rows=None):
    shape = top.shape if chunk is None else (2, rows, LANES)
    guard = own is not None
    flops = 2 * shape[2] * 2 * sum(3 * f.size // 2 for f in factors)
    return pl.pallas_call(
        functools.partial(tick_kernel, guard, guard_all, chunk),
        in_specs=[VMEM] * (5 + guard),
        out_specs=[VMEM] * 2,
        out_shape=[jax.ShapeDtypeStruct(shape, F32)] * 2,
        cost_estimate=pl.CostEstimate(
            flops=flops, transcendentals=0, bytes_accessed=sum(f.size * 2 for f in factors)
        ),
        compiler_params=limit(8),
    )(*([own] if guard else []), top, low, *factors)


def finish_kernel(chunks, first_tail, aliased, *refs):
    if aliased:
        _, *refs = refs
    *ins, out_ref, held, sem = refs
    section = lax.axis_index("rows")
    rows = out_ref.shape[1] // 2
    parts = []
    for at, tail in enumerate(ins[2 * len(chunks) :]):
        parts.append((tail, first_tail + at, rows))
    for at, c in enumerate(chunks):
        held[at] = jnp.where(section > 0, ins[at][...], ins[len(chunks) + at][...])
        parts.append((held.at[at], c, 0))
    copies = [
        pltpu.make_async_copy(
            source, out_ref.at[:, pl.ds(row, rows), pl.ds(c * LANES, LANES)], sem.at[at]
        )
        for at, (source, c, row) in enumerate(parts)
    ]
    for copy in copies:
        copy.start()
    for copy in copies:
        copy.wait()


def finish(out, shape, chunks, given, own, tails, first_tail):
    aliased = out is not None
    operands = [*([out] if aliased else []), *given, *own, *tails]
    return pl.pallas_call(
        functools.partial(finish_kernel, chunks, first_tail, aliased),
        in_specs=[HBM] * aliased + [VMEM] * (len(operands) - aliased),
        out_specs=HBM,
        out_shape=jax.ShapeDtypeStruct(shape, F32),
        scratch_shapes=[
            pltpu.VMEM((max(len(chunks), 1), *operands[-1].shape), F32),
            pltpu.SemaphoreType.DMA((len(chunks) + len(tails),)),
        ],
        input_output_aliases={0: 0} if aliased else {},
        compiler_params=limit(4),
        name="finish",
    )(*operands)


def from_behind(block, distance):
    devices = range(lax.axis_size("rows"))
    route = [(i - distance, i) for i in devices if i - distance in devices]
    return lax.ppermute(block, "rows", route)


def exchange(block, mask):
    return lax.ppermute(block, "cols", [(i, i ^ mask) for i in range(lax.axis_size("cols"))])


def shards(eigenvectors, reflectors, tri_factors, block_order):
    ticks = reflectors.shape[1]
    v_rows = reflectors.shape[3]
    band = reflectors.shape[4]
    chunks = eigenvectors.shape[2] // LANES
    members = lax.axis_size("cols")
    masks = [1 << b for b in reversed(range(members.bit_length() - 1))]

    groups = [[0], [1], list(range(2, ticks))]
    operands = (block_order, reflectors, tri_factors)
    (first,) = pack(*operands, groups[:1])
    *rest, everything = pack(*operands, groups[1:] + [list(range(ticks))])
    gathered = []
    for own in [first, *rest]:
        pieces = [(0, own)]
        for mask in masks[:-1]:
            pieces = pieces + [(o ^ mask, exchange(p, mask)) for o, p in pieces]
        gathered.append(pieces)
    partner = exchange(everything, masks[-1])

    def blocks_of(group):
        pieces = gathered[group]
        far = [(o ^ masks[-1], exchange(p, masks[-1])) for o, p in pieces[1:]]
        return pieces + far

    def factors_of(tick, blocks, at):
        places = [(o, at) for o, _ in blocks] + [(masks[-1], tick)]
        return prep([p for _, p in blocks] + [partner], places, v_rows)

    heads, tails = [None] * chunks, [None] * chunks
    given = [None] * chunks
    for tick in range(ticks):
        if tick < 3:
            blocks = blocks_of(tick)
        factors = factors_of(tick, blocks, max(tick - 2, 0))
        for c in range(chunks):
            if tick == 0:
                heads[c], tails[c] = tick_call(
                    factors, eigenvectors, eigenvectors, chunk=c, rows=band
                )
            elif tick % 2 == 0:
                heads[c], tails[c] = tick_call(factors, given[c], tails[c], own=heads[c])
            else:
                tails[c], back = tick_call(factors, tails[c], given[c], guard_all=True)
            if tick % 2 == 0:
                given[c] = from_behind(heads[c], -1)
            else:
                given[c] = from_behind(back, 1)
    shape = eigenvectors.shape
    early = list(range(chunks - 1))
    out = finish(None, shape, [], [], [], tails[:-1], 0)
    out = finish(out, shape, early, given[:-1], heads[:-1], tails[-1:], chunks - 1)
    return finish(out, shape, [chunks - 1], given[-1:], heads[-1:], [], 0)


def solution(mesh):
    return jax.shard_map(
        shards,
        mesh=mesh,
        in_specs=(
            P(None, "rows", "cols"),
            P("rows", None, None, "cols", None),
            P("rows", None, None, "cols", None),
            P("rows", None),
        ),
        out_specs=P(None, "rows", "cols"),
        check_vma=False,
    )
```

```python
import functools

import jax
import jax.numpy as jnp
from jax import lax
from jax.experimental import pallas as pl
from jax.experimental.pallas import tpu as pltpu
from jax.sharding import PartitionSpec as P

LANES = 128
BF16 = jnp.bfloat16
F32 = jnp.float32


def split(x):
    hi = x.astype(BF16)
    return hi, (x - hi.astype(F32)).astype(BF16)


VMEM = pl.BlockSpec(memory_space=pltpu.VMEM)
HBM = pl.BlockSpec(memory_space=pltpu.HBM)


def limit(mib):
    return pltpu.CompilerParams(vmem_limit_bytes=mib << 20)


def pack_kernel(groups, order_hbm, v_ref, f_ref, *refs):
    outs, (order_ref, order_sem, sem) = refs[:-3], refs[-3:]
    rows = v_ref.shape[3]
    fetch = pltpu.make_async_copy(order_hbm, order_ref, order_sem)
    fetch.start()
    fetch.wait()
    copies = []
    for group, out in zip(groups, outs):
        for at, t in enumerate(group):
            k = order_ref[0, t]
            for source, part in ((v_ref, slice(0, rows)), (f_ref, slice(rows, None))):
                copies.append(
                    pltpu.make_async_copy(
                        source.at[0, k], out.at[at, :, part], sem.at[len(copies)]
                    )
                )
    for copy in copies:
        copy.start()
    for copy in copies:
        copy.wait()


def pack(order, reflectors, tri_factors, groups):
    _, _, two, v_rows, band = reflectors.shape
    shape = (two, v_rows + tri_factors.shape[3], band)
    return pl.pallas_call(
        functools.partial(pack_kernel, groups),
        in_specs=[HBM, HBM, HBM],
        out_specs=[VMEM for _ in groups],
        out_shape=[jax.ShapeDtypeStruct((len(g), *shape), F32) for g in groups],
        scratch_shapes=[
            pltpu.SMEM(order.shape, jnp.int32),
            pltpu.SemaphoreType.DMA,
            pltpu.SemaphoreType.DMA((2 * sum(map(len, groups)),)),
        ],
        compiler_params=limit(1),
        name="pack",
    )(*(pltpu.with_memory_space_constraint(x, pltpu.HBM) for x in (order, reflectors, tri_factors)))


def place(swapped):
    row, col = lax.axis_index("rows"), lax.axis_index("cols")
    if not swapped:
        return row, col
    low = lambda of, bit: lax.bitwise_or(of - lax.bitwise_and(of, 1), lax.bitwise_and(bit, 1))
    return low(row, col), low(col, row)


def prep_kernel(places, v_rows, swapped, *refs):
    pieces, (vt_ref, vd_ref, ff_ref) = refs[: len(places)], refs[len(places) :]
    half = vd_ref.shape[0] // 2
    band = ff_ref.shape[0] // 2
    f_rows = pieces[0].shape[2] - v_rows
    _, me = place(swapped)
    for (offset, at), piece in zip(places, pieces):
        shard = lax.bitwise_xor(me, offset)
        v_at = pl.multiple_of(shard * v_rows, v_rows)
        f_at = pl.multiple_of(shard * f_rows, f_rows)
        row = f_at + lax.broadcasted_iota(jnp.int32, (f_rows, band), 0)
        upper = lax.broadcasted_iota(jnp.int32, (f_rows, band), 1) >= row
        for part in range(2):
            lanes = slice(part * band, (part + 1) * band)
            hi, lo = split(piece[at, part, :v_rows])
            vd_ref[pl.ds(v_at, v_rows), lanes] = hi
            vd_ref[pl.ds(half + v_at, v_rows), lanes] = lo
            hi, lo = split(jnp.where(upper, piece[at, part, v_rows:], 0.0))
            ff_ref[pl.ds(f_at, f_rows), lanes] = hi
            ff_ref[pl.ds(band + f_at, f_rows), lanes] = lo
    for level in range(2):
        for part in range(2):
            block = vd_ref[level * half : (level + 1) * half, part * band : (part + 1) * band]
            vt_ref[level * band : (level + 1) * band, part * half : (part + 1) * half] = block.T


def prep(pieces, places, v_rows, swapped):
    band = pieces[0].shape[3]
    half = v_rows * len(pieces)
    shapes = [(2 * band, 2 * half), (2 * half, 2 * band), (2 * band, 2 * band)]
    return pl.pallas_call(
        functools.partial(prep_kernel, places, v_rows, swapped),
        in_specs=[VMEM for _ in pieces],
        out_specs=[VMEM for _ in shapes],
        out_shape=[jax.ShapeDtypeStruct(s, BF16) for s in shapes],
        compiler_params=limit(2),
        name="prep",
    )(*pieces)


def times(left_ref, right):
    rows = left_ref.shape[0] // 2
    hi, lo = split(right)
    both = jnp.dot(left_ref[...], hi, preferred_element_type=F32)
    return both[:rows] + both[rows:] + jnp.dot(left_ref[:rows], lo, preferred_element_type=F32)


def tick_kernel(odd, swapped, chunk, *refs):
    top_ref, low_ref, vt_ref, vd_ref, ff_ref, *refs = refs
    top_out, low_out = refs[-2:]
    if chunk is not None:
        rows = top_out.shape[1]
        lanes = slice(chunk * LANES, (chunk + 1) * LANES)
        top, low = top_ref[:, :rows, lanes], low_ref[:, rows:, lanes]
    else:
        top, low = top_ref[...], low_ref[...]
    rows, lanes = top.shape[1:]
    re = jnp.concatenate([top[0], low[0]], axis=0)
    im = jnp.concatenate([top[1], low[1]], axis=0)
    w = times(
        vt_ref,
        jnp.concatenate(
            [jnp.concatenate([re, im], axis=1), jnp.concatenate([im, -re], axis=1)], axis=0
        ),
    )

    def rotate(x):
        return jnp.concatenate(
            [x, jnp.concatenate([-x[:, lanes:], x[:, :lanes]], axis=1)], axis=0
        )

    u = times(ff_ref, rotate(w))
    d = times(vd_ref, rotate(u))
    if odd:
        section, _ = place(swapped)
        d = jnp.where(section < lax.axis_size("rows") - 1, d, 0.0)
    top_out[0] = top[0] - d[:rows, :lanes]
    top_out[1] = top[1] - d[:rows, lanes:]
    low_out[0] = low[0] - d[rows:, :lanes]
    low_out[1] = low[1] - d[rows:, lanes:]


def tick_call(factors, top, low, odd, swapped, chunk=None, rows=None):
    shape = top.shape if chunk is None else (2, rows, LANES)
    flops = 2 * shape[2] * 2 * sum(3 * f.size // 2 for f in factors)
    return pl.pallas_call(
        functools.partial(tick_kernel, odd, swapped, chunk),
        in_specs=[VMEM] * 5,
        out_specs=[VMEM] * 2,
        out_shape=[jax.ShapeDtypeStruct(shape, F32)] * 2,
        cost_estimate=pl.CostEstimate(
            flops=flops, transcendentals=0, bytes_accessed=sum(f.size * 2 for f in factors)
        ),
        compiler_params=limit(8),
    )(top, low, *factors)


def finish_kernel(parts, aliased, *refs):
    if aliased:
        _, *refs = refs
    *ins, out_ref, sem = refs
    rows = out_ref.shape[1] // 2
    copies = [
        pltpu.make_async_copy(
            source, out_ref.at[:, pl.ds(half * rows, rows), pl.ds(c * LANES, LANES)], sem.at[at]
        )
        for at, (source, (half, c)) in enumerate(zip(ins, parts))
    ]
    for copy in copies:
        copy.start()
    for copy in copies:
        copy.wait()


def finish(out, shape, blocks):
    aliased = out is not None
    operands = [*([out] if aliased else []), *(b for _, b in blocks)]
    return pl.pallas_call(
        functools.partial(finish_kernel, tuple(p for p, _ in blocks), aliased),
        in_specs=[HBM] * aliased + [VMEM] * len(blocks),
        out_specs=HBM,
        out_shape=jax.ShapeDtypeStruct(shape, F32),
        scratch_shapes=[pltpu.SemaphoreType.DMA((len(blocks),))],
        input_output_aliases={0: 0} if aliased else {},
        compiler_params=limit(4),
        name="finish",
    )(*operands)


def plain(section, block):
    return section, block


def swapped(section, block):
    return section - section % 2 + block % 2, block - block % 2 + section % 2


def move(value, source, target, step=0, flip=0):
    sections, blocks = lax.axis_size("rows"), lax.axis_size("cols")
    flat = lambda at: at[0] * blocks + at[1]
    route = [
        (flat(source(s, b)), flat(target((s + step) % sections, b ^ flip)))
        for s in range(sections)
        for b in range(blocks)
    ]
    return lax.ppermute(value, ("rows", "cols"), route)


def exchange(block, mask):
    return lax.ppermute(block, "cols", [(i, i ^ mask) for i in range(lax.axis_size("cols"))])


def shards(eigenvectors, reflectors, tri_factors, block_order):
    v_rows = reflectors.shape[3]
    band = reflectors.shape[4]
    chunks = eigenvectors.shape[2] // LANES
    members = lax.axis_size("cols")
    masks = [1 << b for b in reversed(range(members.bit_length() - 1))]

    operands = (block_order, reflectors, tri_factors)
    own = [None] * 4
    (own[0],) = pack(*operands, [[0]])
    own[2], own[3] = pack(*operands, [[2], [3]])
    own[1], both = pack(*operands, [[1], [0, 1]])
    partner = exchange(both, masks[-1])
    factors = []
    for tick in range(4):
        pieces = [(0, own[tick])]
        if tick >= 2:
            pieces = [(f, move(own[tick], plain, swapped, flip=f)) for f in (0, masks[-1])]
        for mask in masks[:-1]:
            pieces = pieces + [(o ^ mask, exchange(p, mask)) for o, p in pieces]
        if tick < 2:
            pieces += [(o ^ masks[-1], exchange(p, masks[-1])) for o, p in pieces[1:]]
        places = [(o, 0) for o, _ in pieces]
        pieces = [p for _, p in pieces]
        if tick < 2:
            places, pieces = places + [(masks[-1], tick)], pieces + [partner]
        factors.append(prep(pieces, places, v_rows, tick >= 2))

    blocks = []
    for c in range(chunks):
        head, tail = tick_call(
            factors[0], eigenvectors, eigenvectors, False, False, chunk=c, rows=band
        )
        head = move(head, plain, plain, -1)
        tail, head = tick_call(factors[1], tail, head, True, False)
        tail = move(tail, plain, swapped)
        head = move(head, plain, swapped, 1)
        head, tail = tick_call(factors[2], head, tail, False, True)
        head = move(head, swapped, swapped, -1)
        tail, head = tick_call(factors[3], tail, head, True, True)
        tail = move(tail, swapped, plain)
        head = move(head, swapped, plain, 1)
        blocks.append([((1, c), tail), ((0, c), head)])
    out = finish(None, eigenvectors.shape, sum(blocks[:-1], []))
    return finish(out, eigenvectors.shape, blocks[-1])


def solution(mesh):
    return jax.shard_map(
        shards,
        mesh=mesh,
        in_specs=(
            P(None, "rows", "cols"),
            P("rows", None, None, "cols", None),
            P("rows", None, None, "cols", None),
            P("rows", None),
        ),
        out_specs=P(None, "rows", "cols"),
        check_vma=False,
    )
```

```python
import functools

import jax
import jax.numpy as jnp
from jax import lax
from jax.experimental import pallas as pl
from jax.experimental.pallas import tpu as pltpu
from jax.sharding import PartitionSpec as P

LANES = 128
BF16 = jnp.bfloat16
F32 = jnp.float32


def split(x):
    hi = x.astype(BF16)
    return hi, (x - hi.astype(F32)).astype(BF16)


VMEM = pl.BlockSpec(memory_space=pltpu.VMEM)
HBM = pl.BlockSpec(memory_space=pltpu.HBM)


def limit(mib):
    return pltpu.CompilerParams(vmem_limit_bytes=mib << 20)


def pack_kernel(groups, order_hbm, v_ref, f_ref, *refs):
    outs, (order_ref, order_sem, sem) = refs[:-3], refs[-3:]
    rows = v_ref.shape[3]
    fetch = pltpu.make_async_copy(order_hbm, order_ref, order_sem)
    fetch.start()
    fetch.wait()
    copies = []
    for group, out in zip(groups, outs):
        for at, t in enumerate(group):
            k = order_ref[0, t]
            for source, part in ((v_ref, slice(0, rows)), (f_ref, slice(rows, None))):
                copies.append(
                    pltpu.make_async_copy(
                        source.at[0, k], out.at[at, :, part], sem.at[len(copies)]
                    )
                )
    for copy in copies:
        copy.start()
    for copy in copies:
        copy.wait()


def pack(order, reflectors, tri_factors, groups):
    _, _, two, v_rows, band = reflectors.shape
    shape = (two, v_rows + tri_factors.shape[3], band)
    return pl.pallas_call(
        functools.partial(pack_kernel, groups),
        in_specs=[HBM, HBM, HBM],
        out_specs=[VMEM for _ in groups],
        out_shape=[jax.ShapeDtypeStruct((len(g), *shape), F32) for g in groups],
        scratch_shapes=[
            pltpu.SMEM(order.shape, jnp.int32),
            pltpu.SemaphoreType.DMA,
            pltpu.SemaphoreType.DMA((2 * sum(map(len, groups)),)),
        ],
        compiler_params=limit(1),
        name="pack",
    )(*(pltpu.with_memory_space_constraint(x, pltpu.HBM) for x in (order, reflectors, tri_factors)))


def place(swapped):
    row, col = lax.axis_index("rows"), lax.axis_index("cols")
    if not swapped:
        return row, col
    low = lambda of, bit: lax.bitwise_or(of - lax.bitwise_and(of, 1), lax.bitwise_and(bit, 1))
    return low(row, col), low(col, row)


def prep_kernel(places, v_rows, swapped, *refs):
    pieces, (vt_ref, vd_ref, ff_ref) = refs[: len(places)], refs[len(places) :]
    half = vd_ref.shape[0] // 2
    band = ff_ref.shape[0] // 2
    f_rows = pieces[0].shape[2] - v_rows
    _, me = place(swapped)
    for (offset, at), piece in zip(places, pieces):
        shard = lax.bitwise_xor(me, offset)
        v_at = pl.multiple_of(shard * v_rows, v_rows)
        f_at = pl.multiple_of(shard * f_rows, f_rows)
        row = f_at + lax.broadcasted_iota(jnp.int32, (f_rows, band), 0)
        upper = lax.broadcasted_iota(jnp.int32, (f_rows, band), 1) >= row
        for part in range(2):
            lanes = slice(part * band, (part + 1) * band)
            hi, lo = split(piece[at, part, :v_rows])
            vd_ref[pl.ds(v_at, v_rows), lanes] = hi
            vd_ref[pl.ds(half + v_at, v_rows), lanes] = lo
            hi, lo = split(jnp.where(upper, piece[at, part, v_rows:], 0.0))
            ff_ref[pl.ds(f_at, f_rows), lanes] = hi
            ff_ref[pl.ds(band + f_at, f_rows), lanes] = lo
    for level in range(2):
        for part in range(2):
            block = vd_ref[level * half : (level + 1) * half, part * band : (part + 1) * band]
            vt_ref[level * band : (level + 1) * band, part * half : (part + 1) * half] = block.T


def prep(pieces, places, v_rows, swapped):
    band = pieces[0].shape[3]
    half = v_rows * len(pieces)
    shapes = [(2 * band, 2 * half), (2 * half, 2 * band), (2 * band, 2 * band)]
    return pl.pallas_call(
        functools.partial(prep_kernel, places, v_rows, swapped),
        in_specs=[VMEM for _ in pieces],
        out_specs=[VMEM for _ in shapes],
        out_shape=[jax.ShapeDtypeStruct(s, BF16) for s in shapes],
        compiler_params=limit(2),
        name="prep",
    )(*pieces)


def times(left_ref, right):
    rows = left_ref.shape[0] // 2
    hi, lo = split(right)
    both = jnp.dot(left_ref[...], hi, preferred_element_type=F32)
    return both[:rows] + both[rows:] + jnp.dot(left_ref[:rows], lo, preferred_element_type=F32)


def tick_kernel(odd, swapped, chunk, *refs):
    top_ref, low_ref, vt_ref, vd_ref, ff_ref, *refs = refs
    top_out, low_out = refs[-2:]
    if chunk is not None:
        rows = top_out.shape[1]
        lanes = slice(chunk * LANES, (chunk + 1) * LANES)
        top, low = top_ref[:, :rows, lanes], low_ref[:, rows:, lanes]
    else:
        top, low = top_ref[...], low_ref[...]
    rows, lanes = top.shape[1:]
    re = jnp.concatenate([top[0], low[0]], axis=0)
    im = jnp.concatenate([top[1], low[1]], axis=0)
    w = times(
        vt_ref,
        jnp.concatenate(
            [jnp.concatenate([re, im], axis=1), jnp.concatenate([im, -re], axis=1)], axis=0
        ),
    )

    def rotate(x):
        return jnp.concatenate(
            [x, jnp.concatenate([-x[:, lanes:], x[:, :lanes]], axis=1)], axis=0
        )

    u = times(ff_ref, rotate(w))
    d = times(vd_ref, rotate(u))
    if odd:
        section, _ = place(swapped)
        d = jnp.where(section < lax.axis_size("rows") - 1, d, 0.0)
    top_out[0] = top[0] - d[:rows, :lanes]
    top_out[1] = top[1] - d[:rows, lanes:]
    low_out[0] = low[0] - d[rows:, :lanes]
    low_out[1] = low[1] - d[rows:, lanes:]


def tick_call(factors, top, low, odd, swapped, chunk=None, rows=None):
    shape = top.shape if chunk is None else (2, rows, LANES)
    flops = 2 * shape[2] * 2 * sum(3 * f.size // 2 for f in factors)
    return pl.pallas_call(
        functools.partial(tick_kernel, odd, swapped, chunk),
        in_specs=[VMEM] * 5,
        out_specs=[VMEM] * 2,
        out_shape=[jax.ShapeDtypeStruct(shape, F32)] * 2,
        cost_estimate=pl.CostEstimate(
            flops=flops, transcendentals=0, bytes_accessed=sum(f.size * 2 for f in factors)
        ),
        compiler_params=limit(8),
    )(top, low, *factors)


def finish_kernel(parts, aliased, *refs):
    if aliased:
        _, *refs = refs
    *ins, out_ref, sem = refs
    rows = out_ref.shape[1] // 2
    copies = [
        pltpu.make_async_copy(
            source, out_ref.at[:, pl.ds(half * rows, rows), pl.ds(c * LANES, LANES)], sem.at[at]
        )
        for at, (source, (half, c)) in enumerate(zip(ins, parts))
    ]
    for copy in copies:
        copy.start()
    for copy in copies:
        copy.wait()


def finish(out, shape, blocks):
    aliased = out is not None
    operands = [*([out] if aliased else []), *(b for _, b in blocks)]
    return pl.pallas_call(
        functools.partial(finish_kernel, tuple(p for p, _ in blocks), aliased),
        in_specs=[HBM] * aliased + [VMEM] * len(blocks),
        out_specs=HBM,
        out_shape=jax.ShapeDtypeStruct(shape, F32),
        scratch_shapes=[pltpu.SemaphoreType.DMA((len(blocks),))],
        input_output_aliases={0: 0} if aliased else {},
        compiler_params=limit(4),
        name="finish",
    )(*operands)


def plain(section, block):
    return section, block


def swapped(section, block):
    return section - section % 2 + block % 2, block - block % 2 + section % 2


def move(value, source, target, step=0, flip=0):
    sections, blocks = lax.axis_size("rows"), lax.axis_size("cols")
    flat = lambda at: at[0] * blocks + at[1]
    route = [
        (flat(source(s, b)), flat(target((s + step) % sections, b ^ flip)))
        for s in range(sections)
        for b in range(blocks)
    ]
    return lax.ppermute(value, ("rows", "cols"), route)


def exchange(block, mask):
    return lax.ppermute(block, "cols", [(i, i ^ mask) for i in range(lax.axis_size("cols"))])


def shards(eigenvectors, reflectors, tri_factors, block_order):
    v_rows = reflectors.shape[3]
    band = reflectors.shape[4]
    chunks = eigenvectors.shape[2] // LANES
    members = lax.axis_size("cols")
    masks = [1 << b for b in reversed(range(members.bit_length() - 1))]

    operands = (block_order, reflectors, tri_factors)
    own = [None] * 4
    own[0], own[2] = pack(*operands, [[0], [2]])
    own[3], own[1], both = pack(*operands, [[3], [1], [0, 1]])
    partner = exchange(both, masks[-1])
    factors = []
    for tick in range(4):
        pieces = [(0, own[tick])]
        if tick >= 2:
            pieces = []
            for flip in (0, masks[-1]):
                pieces.append((flip, move(own[tick], plain, swapped, flip=flip)))
        spread = []
        for piece in pieces:
            group = [piece]
            for mask in masks[:-1]:
                group = group + [(o ^ mask, exchange(p, mask)) for o, p in group]
            spread += group
        pieces = spread
        if tick < 2:
            pieces += [(o ^ masks[-1], exchange(p, masks[-1])) for o, p in pieces[1:]]
        places = [(o, 0) for o, _ in pieces]
        pieces = [p for _, p in pieces]
        if tick < 2:
            places, pieces = places + [(masks[-1], tick)], pieces + [partner]
        factors.append(prep(pieces, places, v_rows, tick >= 2))

    blocks = []
    for c in range(chunks):
        head, tail = tick_call(
            factors[0], eigenvectors, eigenvectors, False, False, chunk=c, rows=band
        )
        head = move(head, plain, plain, -1)
        tail, head = tick_call(factors[1], tail, head, True, False)
        tail = move(tail, plain, swapped)
        head = move(head, plain, swapped, 1)
        head, tail = tick_call(factors[2], head, tail, False, True)
        head = move(head, swapped, swapped, -1)
        tail, head = tick_call(factors[3], tail, head, True, True)
        tail = move(tail, swapped, plain)
        head = move(head, swapped, plain, 1)
        blocks.append([((1, c), tail), ((0, c), head)])
    out = finish(None, eigenvectors.shape, sum(blocks[:-1], []))
    return finish(out, eigenvectors.shape, blocks[-1])


def solution(mesh):
    return jax.shard_map(
        shards,
        mesh=mesh,
        in_specs=(
            P(None, "rows", "cols"),
            P("rows", None, None, "cols", None),
            P("rows", None, None, "cols", None),
            P("rows", None),
        ),
        out_specs=P(None, "rows", "cols"),
        check_vma=False,
    )
```
